32 devices in a mesh: occa: 4 (over x, core), occb: 4 (over z), rows: 2 (over y).
Axes of the slice: x: 2, y: 2, z: 4, core: 2. Of those that a mesh axis runs over, the one named last changes fastest.
Arguments:
- density: float32 [512, 4, 4, 2, 512], P('rows', 'occa', 'occb'), may hold values from -6 to 6
- operators: float32 [5, 512, 512], P(None, 'rows'), as said below
- rates: float32 [2], replicated, may hold values from 0.05 to 0.5
- coupling: float32 [2, 2], replicated, may hold values from 0.3 to 1
- keep_mask: int32 [4, 4], P('occa', 'occb'), may hold values 0 or 1
Outputs:
- advanced: float32 [512, 4, 4, 2, 512], P('rows', 'occa', 'occb')
The draws below stay inside these ranges and needn't reach their ends.
Inputs may be any that keep to these rules, and one draw needn't show every extreme that they name: `keep_mask`: 1 keeps an auxiliary matrix in the hierarchy, 0 removes it. `operators`: each of the five matrices is symmetric.
All inputs are finite; a program needn't handle non-finite values. No bound on the sum of `keep_mask` on one device may be relied on, other than what follows from the above.
Results may differ from the reference program's by a relative error of at most 0.00005.
Values sent between devices are 32-bit elements; how exact they have to be, the bound alone decides.
No kernel may reach another device: no remote copies, remote signals or barrier semaphores. Data moves between devices by JAX's collectives and lax.ppermute only.
A program may use at most 64 MiB of HBM per device.

```python
import math
import jax
import jax.numpy as jnp
from jax import lax

M = 512
NA = 4
NB = 4


def draw_operators(key, part):
    sampled = jax.random.normal(key, (5, M, M), jnp.float32)
    return (sampled + jnp.swapaxes(sampled, 1, 2)) / jnp.sqrt(2.0 * M)


def place_ends(values, own_key, low, high):
    extent = values.shape
    place = [jax.random.randint(jax.random.fold_in(own_key, axis), (), 0, extent[axis]) for axis in range(len(extent))]
    values = values.at[tuple(place)].set(low)
    longest = extent.index(max(extent))
    place[longest] = (place[longest] + 1) % extent[longest]
    return values.at[tuple(place)].set(high)


def levels(key, extent, shards, smallest, high):
    gain, own = 1.0, jax.random.fold_in(key, 6)
    for dim, parts in shards:
        steps = jnp.exp(jax.random.uniform(jax.random.fold_in(own, dim), (parts,), jnp.float32, smallest / len(shards), high / len(shards)))
        gain = gain * jnp.repeat(steps, extent[dim] // parts).reshape([-1 if axis == dim else 1 for axis in range(len(extent))])
    return gain


def normal_values(rng, dims, scale, reach, pieces=(), held_as=jnp.bfloat16):
    loudness = levels(rng, dims, pieces, -0.22, 0.18) if pieces else 1.0
    array = jax.random.normal(rng, dims, jnp.float32) * scale * loudness
    return jnp.minimum(jnp.maximum(array, -reach), reach).astype(held_as)


def setup_inputs(seed: int = 0) -> dict:
    seeds = jax.random.split(jax.random.key(seed), 6)
    density = normal_values(seeds[0], (M, NA, NB, 2, M), 1.0, 6.0, ((0, 2), (1, 4), (2, 4)), jnp.float32)
    operators = draw_operators(jax.random.fold_in(seeds[5], 71), 0)
    rates = jnp.clip(jnp.exp(jax.random.uniform(seeds[2], (2,), jnp.float32, math.log(0.05), math.log(0.5))), 0.05, 0.5)
    coupling = jnp.clip(jax.random.uniform(seeds[3], (2, 2), jnp.float32, 0.3, 1.0), 0.3, 1.0)
    keep_mask = place_ends((jax.random.randint(seeds[4], (NA, NB), 0, 4) < 3).astype(jnp.int32), jax.random.fold_in(seeds[4], 1), 0, 1)
    return {"density": density, "operators": operators, "rates": rates, "coupling": coupling, "keep_mask": keep_mask}


TIME_STEP = 0.05
PRECISE = lax.Precision.HIGHEST

def neighbours(extended, count_a, count_b):
    return jnp.stack([extended[:, 1:count_a + 1, 1:count_b + 1], extended[:, 2:count_a + 2, 1:count_b + 1], extended[:, 0:count_a, 1:count_b + 1], extended[:, 1:count_a + 1, 2:count_b + 2], extended[:, 1:count_a + 1, 0:count_b]], axis=3)

def ladder_factors(occ_a, occ_b, coupling):
    zeros = jnp.zeros_like(occ_a + occ_b)
    up_a = jnp.sqrt(occ_a + 1.0) + zeros
    up_b = jnp.sqrt(occ_b + 1.0) + zeros
    down_a = jnp.sqrt(occ_a) + zeros
    down_b = jnp.sqrt(occ_b) + zeros
    factor_re = jnp.stack([zeros, zeros, down_a * coupling[0, 1], zeros, down_b * coupling[1, 1]], axis=-1)
    factor_im = jnp.stack([zeros - 1.0, -up_a, -down_a * coupling[0, 0], -up_b, -down_b * coupling[1, 0]], axis=-1)
    return (factor_re, factor_im)

def weighted(stacked, factor_re, factor_im):
    part_re = stacked[..., 0, :]
    part_im = stacked[..., 1, :]
    scale_re = factor_re[None, :, :, :, None]
    scale_im = factor_im[None, :, :, :, None]
    return jnp.stack([scale_re * part_re - scale_im * part_im, scale_re * part_im + scale_im * part_re], axis=4)

def derivative(field, operators, factor_re, factor_im, damping, kept):
    extended = jnp.pad(field, ((0, 0), (1, 1), (1, 1), (0, 0), (0, 0)))
    stacked = neighbours(extended, NA, NB)
    left_ops = weighted(stacked, factor_re, factor_im)
    right_ops = weighted(stacked, factor_re, -factor_im)
    left_part = jnp.einsum('kic,cabkpm->iabpm', operators, left_ops, precision=PRECISE)
    right_part = jnp.einsum('iabkpc,kcm->iabpm', right_ops, operators, precision=PRECISE)
    return (left_part + right_part - damping * field) * kept

def reference(density, operators, rates, coupling, keep_mask):
    occ_a = jnp.arange(NA).astype(jnp.float32)[:, None]
    occ_b = jnp.arange(NB).astype(jnp.float32)[None, :]
    factor_re, factor_im = ladder_factors(occ_a, occ_b, coupling)
    damping = (occ_a * rates[0] + occ_b * rates[1])[None, :, :, None, None]
    kept = keep_mask.astype(jnp.float32)[None, :, :, None, None]
    start = density * kept
    first = derivative(start, operators, factor_re, factor_im, damping, kept)
    second = derivative(first, operators, factor_re, factor_im, damping, kept)
    return start + TIME_STEP * first + 0.5 * TIME_STEP * TIME_STEP * second
```

```python
import functools

import jax
import jax.numpy as jnp
from jax import lax
from jax.experimental import pallas as pl
from jax.experimental.pallas import tpu as pltpu
from jax.sharding import PartitionSpec as P

TIME_STEP = 0.05
PRECISE = lax.Precision.HIGHEST
SLOTS = 5
HALVES = 2
F32 = jnp.float32
BF16 = jnp.bfloat16


def padded(cells, sides, width):
    for axis, dim in sides:
        count = lax.axis_size(axis)
        ends = count - 1
        head = lax.slice_in_dim(cells, 0, width, axis=dim)
        tail = lax.slice_in_dim(cells, cells.shape[dim] - width, cells.shape[dim], axis=dim)
        cells = jnp.concatenate(
            [
                lax.ppermute(tail, axis, [(i, (i + 1) % count) for i in range(ends)]),
                cells,
                lax.ppermute(head, axis, [((i + 1) % count, i) for i in range(ends)]),
            ],
            axis=dim,
        )
    return cells


def neighbours(extended, count_a, count_b):
    return jnp.stack(
        [
            extended[:, 1 : count_a + 1, 1 : count_b + 1],
            extended[:, 2 : count_a + 2, 1 : count_b + 1],
            extended[:, 0:count_a, 1 : count_b + 1],
            extended[:, 1 : count_a + 1, 2 : count_b + 2],
            extended[:, 1 : count_a + 1, 0:count_b],
        ],
        axis=3,
    )


def ladder_factors(occ_a, occ_b, coupling):
    zeros = jnp.zeros_like(occ_a + occ_b)
    up_a = jnp.sqrt(occ_a + 1.0)
    up_b = jnp.sqrt(occ_b + 1.0)
    down_a = jnp.sqrt(occ_a)
    down_b = jnp.sqrt(occ_b)
    factor_re = jnp.stack(
        [zeros, zeros, down_a * coupling[0, 1], zeros, down_b * coupling[1, 1]], axis=-1
    )
    factor_im = jnp.stack(
        [zeros - 1.0, -up_a, -down_a * coupling[0, 0], -up_b, -down_b * coupling[1, 0]], axis=-1
    )
    return (factor_re, factor_im)


def weighted(stacked, factor_re, factor_im):
    part_re = stacked[..., 0, :]
    part_im = stacked[..., 1, :]
    scale_re = factor_re[None, :, :, :, None]
    scale_im = factor_im[None, :, :, :, None]
    return jnp.stack(
        [scale_re * part_re - scale_im * part_im, scale_re * part_im + scale_im * part_re], axis=4
    )


def general_shards(density, operators, rates, coupling, keep_mask):
    row_count = density.shape[0]
    count_a = density.shape[1]
    count_b = density.shape[2]
    full_ops = lax.all_gather(operators, "rows", axis=1, tiled=True)
    occ_a = (lax.axis_index("occa") * count_a + jnp.arange(count_a)).astype(F32)[:, None]
    occ_b = (lax.axis_index("occb") * count_b + jnp.arange(count_b)).astype(F32)[None, :]
    row_start = lax.axis_index("rows") * row_count
    factor_re, factor_im = ladder_factors(occ_a, occ_b, coupling)
    damping = (occ_a * rates[0] + occ_b * rates[1])[None, :, :, None, None]
    kept = keep_mask.astype(F32)[None, :, :, None, None]

    def derivative(field):
        extended = padded(field, (("occa", 1), ("occb", 2)), 1)
        stacked = neighbours(extended, count_a, count_b)
        right_ops = weighted(stacked, factor_re, -factor_im)
        right_part = jnp.einsum("iabkpc,kcm->iabpm", right_ops, full_ops, precision=PRECISE)
        left_ops = weighted(stacked, factor_re, factor_im)
        op_slice = lax.dynamic_slice_in_dim(full_ops, row_start, row_count, 2)
        left_part = lax.psum_scatter(
            jnp.einsum("kic,cabkpm->iabpm", op_slice, left_ops, precision=PRECISE),
            "rows",
            scatter_dimension=0,
            tiled=True,
        )
        return (left_part + right_part - damping * field) * kept

    start = density * kept
    first = derivative(start)
    second = derivative(first)
    return start + TIME_STEP * first + 0.5 * TIME_STEP * TIME_STEP * second


def split(value):
    high = value.astype(BF16)
    return high, (value - high.astype(F32)).astype(BF16)


def three_dots(a_high, a_low, b_high, b_low):
    dot = functools.partial(jnp.dot, preferred_element_type=F32)
    return dot(a_high, b_high) + (dot(a_high, b_low) + dot(a_low, b_high))


def operators_kernel(place, local, lp_high, lp_low, lo_high, lo_low, vr_high, vr_low):
    half = local.shape[1]
    mine = pl.multiple_of(place[0] * half, half)
    theirs = pl.multiple_of((1 - place[0]) * half, half)
    own = local[0, :, pl.ds(mine, half)]
    cross = local[0, :, pl.ds(theirs, half)]
    lo_high[...], lo_low[...] = split(own)
    lp_high[...], lp_low[...] = split(cross.T)
    vr_high[0], vr_low[0] = split(local[0])


def prepare_operators(place, local):
    slots, half, full = local.shape
    wide = jax.ShapeDtypeStruct((half, slots * half), BF16)
    rows = jax.ShapeDtypeStruct((slots, half, full), BF16)
    return pl.pallas_call(
        operators_kernel,
        out_shape=(wide,) * 4 + (rows,) * 2,
        grid_spec=pltpu.PrefetchScalarGridSpec(
            num_scalar_prefetch=1,
            grid=(slots,),
            in_specs=[pl.BlockSpec((1, half, full), lambda k, place: (place[1 + k], 0, 0))],
            out_specs=[pl.BlockSpec((half, half), lambda k, place: (0, k))] * 4
            + [pl.BlockSpec((1, half, full), lambda k, place: (k, 0, 0))] * 2,
        ),
        name="prepare_operators",
    )(place, local)


def far_kernel(place, local, far, vr_high, vr_low):
    half = local.shape[1]
    mine = pl.multiple_of(place[0] * half, half)
    theirs = pl.multiple_of((1 - place[0]) * half, half)
    high, low = split(local[0, :, pl.ds(theirs, half)].T)
    vr_high[0, :, pl.ds(mine, half)] = high
    vr_low[0, :, pl.ds(mine, half)] = low
    high, low = split(far[0])
    vr_high[0, :, pl.ds(theirs, half)] = high
    vr_low[0, :, pl.ds(theirs, half)] = low


def prepare_far(place, local, far):
    slots, half, full = local.shape
    rows = jax.ShapeDtypeStruct((slots, half, full), BF16)
    return pl.pallas_call(
        far_kernel,
        out_shape=(rows,) * 2,
        grid_spec=pltpu.PrefetchScalarGridSpec(
            num_scalar_prefetch=1,
            grid=(slots,),
            in_specs=[
                pl.BlockSpec((1, half, full), lambda k, place: (place[1 + k], 0, 0)),
                pl.BlockSpec((1, half, half), lambda k, place: (place[1 + k], 0, 0)),
            ],
            out_specs=[pl.BlockSpec((1, half, full), lambda k, place: (k, 0, 0))] * 2,
        ),
        name="prepare_far",
    )(place, local, far)


def left_terms(factors, fields, w_high, w_low):
    half, width = fields[0].shape[1:]
    for slot, field in enumerate(fields):
        re, im = field[0], field[1]
        scale_re, scale_im = factors[slot], factors[SLOTS + slot]
        rows = pl.ds(slot * half, half)
        w_high[rows, :width], w_low[rows, :width] = split(scale_re * re - scale_im * im)
        w_high[rows, width:], w_low[rows, width:] = split(scale_re * im + scale_im * re)


def right_terms(factors, fields, z_high, z_low):
    half, width = fields[0].shape[1:]
    for slot, field in enumerate(fields):
        re, im = field[0], field[1]
        scale_re, scale_im = factors[slot], factors[SLOTS + slot]
        columns = pl.ds(slot * width, width)
        z_high[:half, columns], z_low[:half, columns] = split(scale_re * re + scale_im * im)
        z_high[half:, columns], z_low[half:, columns] = split(scale_re * im - scale_im * re)


def send_kernel(factors, f0, f1, f2, f3, f4, lp_high, lp_low, out, w_high, w_low):
    width = f0.shape[2]
    left_terms(factors, (f0, f1, f2, f3, f4), w_high, w_low)
    part = three_dots(lp_high[...], lp_low[...], w_high[...], w_low[...])
    out[0] = part[:, :width]
    out[1] = part[:, width:]


def keep_kernel(
    half_index, has_sum, factors, f0, f1, f2, f3, f4, lo_high, lo_low, vr_high, vr_low, *rest
):
    before, (out, w_high, w_low, z_high, z_low) = (rest[:1], rest[1:]) if has_sum else ((), rest)
    fields = (f0, f1, f2, f3, f4)
    half, width = f0.shape[1:]
    left_terms(factors, fields, w_high, w_low)
    right_terms(factors, fields, z_high, z_low)
    slots_rows = SLOTS * width
    far_high = vr_high[...].reshape(slots_rows, vr_high.shape[2])
    far_low = vr_low[...].reshape(slots_rows, vr_low.shape[2])
    right = three_dots(z_high[...], z_low[...], far_high, far_low)
    left = three_dots(lo_high[...], lo_low[...], w_high[...], w_low[...])
    for block in range(HALVES):
        for part in range(2):
            total = right[part * half : (part + 1) * half, block * width : (block + 1) * width]
            if block == half_index:
                total = total + left[:, part * width : (part + 1) * width]
            if has_sum:
                total = total + before[0][block, part]
            out[block, part] = total


VMEM_SPEC = pl.BlockSpec(memory_space=pltpu.VMEM)
SMEM_SPEC = pl.BlockSpec(memory_space=pltpu.SMEM)


def send_part(factors, fields, lp):
    _, half, width = fields[0].shape
    deep = SLOTS * half
    return pl.pallas_call(
        send_kernel,
        out_shape=jax.ShapeDtypeStruct((2, half, width), F32),
        in_specs=[SMEM_SPEC] + [VMEM_SPEC] * (SLOTS + 2),
        out_specs=VMEM_SPEC,
        scratch_shapes=[pltpu.VMEM((deep, 2 * width), BF16)] * 2,
        cost_estimate=pl.CostEstimate(
            flops=6 * half * deep * 2 * width, bytes_accessed=4 << 20, transcendentals=0
        ),
        name="send_part",
    )(factors, *fields, *lp)


def keep_part(half_index, factors, fields, lo, vr, before=None):
    _, half, width = fields[0].shape
    deep = SLOTS * half
    extra = () if before is None else (before,)
    return pl.pallas_call(
        functools.partial(keep_kernel, half_index, before is not None),
        out_shape=jax.ShapeDtypeStruct((HALVES, 2, half, width), F32),
        in_specs=[SMEM_SPEC] + [VMEM_SPEC] * (SLOTS + 4 + len(extra)),
        out_specs=VMEM_SPEC,
        scratch_shapes=[pltpu.VMEM((deep, 2 * width), BF16)] * 2
        + [pltpu.VMEM((2 * half, SLOTS * width), BF16)] * 2,
        cost_estimate=pl.CostEstimate(
            flops=18 * half * deep * 2 * width, bytes_accessed=8 << 20, transcendentals=0
        ),
        name="keep_part",
    )(factors, *fields, *lo, *vr, *extra)


def paired_shards(density, operators, rates, coupling, keep_mask):
    rows = density.shape[0]
    full = density.shape[4]
    width = full // HALVES
    count_a, count_b = lax.axis_size("occa"), lax.axis_size("occb")
    at_a, at_b, at_row = lax.axis_index("occa"), lax.axis_index("occb"), lax.axis_index("rows")
    even = at_a % 2 == 0
    kept = keep_mask.astype(F32)[0, 0]

    swap_rows = [(0, 1), (1, 0)]
    pairs = [(i, i + 1) for i in range(0, count_a, 2)]
    swap_in = pairs + [(j, i) for i, j in pairs]
    gaps = [(i, i + 1) for i in range(1, count_a - 1, 2)]
    swap_out = gaps + [(j, i) for i, j in gaps]
    upward = [(i, i + 1) for i in range(count_b - 1)]
    downward = [(j, i) for i, j in upward]

    occ_a, occ_b = at_a.astype(F32), at_b.astype(F32)
    up_a, up_b = jnp.sqrt(occ_a + 1.0), jnp.sqrt(occ_b + 1.0)
    down_a, down_b = jnp.sqrt(occ_a), jnp.sqrt(occ_b)
    zero = jnp.zeros((), F32)
    above = (zero, -up_a)
    below = (down_a * coupling[0, 1], -down_a * coupling[0, 0])
    near = [jnp.where(even, u, d) for u, d in zip(above, below)]
    far = [jnp.where(even, d, u) for u, d in zip(above, below)]
    factors = jnp.stack(
        [zero, near[0], far[0], zero, down_b * coupling[1, 1]]
        + [zero - 1.0, near[1], far[1], -up_b, -down_b * coupling[1, 0]]
    )
    damping = occ_a * rates[0] + occ_b * rates[1]
    one = jnp.ones((), jnp.int32)
    near_op = jnp.where(even, 1, 2).astype(jnp.int32)
    place = jnp.stack([at_row.astype(jnp.int32), 0 * one, near_op, 3 - near_op, 3 * one, 4 * one])

    planes = jnp.transpose(density.reshape(rows, 2, full), (1, 0, 2)) * kept
    start = [planes[:, :, m * width : (m + 1) * width] for m in range(HALVES)]

    own_block = lax.dynamic_slice_in_dim(operators, at_row * rows, rows, 2)
    piece = lax.dynamic_slice_in_dim(own_block, (at_a % 2) * (rows // 2), rows // 2, 1)
    piece = lax.ppermute(piece, "rows", swap_rows)
    other = lax.ppermute(piece, "occa", swap_in)
    far_block = jnp.concatenate(
        [jnp.where(even, piece, other), jnp.where(even, other, piece)], axis=1
    )

    lp_high, lp_low, lo_high, lo_low, own_high, own_low = prepare_operators(place, operators)
    far_high, far_low = prepare_far(place, operators, far_block)
    first_row = at_row == 0
    vr = [
        [jnp.where(first_row, own_high, far_high), jnp.where(first_row, own_low, far_low)],
        [jnp.where(first_row, far_high, own_high), jnp.where(first_row, far_low, own_low)],
    ]

    def derivative(field):
        total = None
        arrived = []
        for m in range(HALVES):
            x = field[m]
            fields = (
                x,
                lax.ppermute(x, "occa", swap_in),
                lax.ppermute(x, "occa", swap_out),
                lax.ppermute(x, "occb", downward),
                lax.ppermute(x, "occb", upward),
            )
            sent = send_part(factors, fields, (lp_high, lp_low))
            arrived.append(lax.ppermute(sent, "rows", swap_rows))
            total = keep_part(m, factors, fields, (lo_high, lo_low), vr[m], total)
        return [
            (total[m] + arrived[m] - damping * field[m]) * kept for m in range(HALVES)
        ]

    first = derivative(start)
    second = derivative(first)
    result = [
        start[m] + TIME_STEP * first[m] + 0.5 * TIME_STEP * TIME_STEP * second[m]
        for m in range(HALVES)
    ]
    result = jnp.transpose(jnp.concatenate(result, axis=2), (1, 0, 2))
    return result.reshape(density.shape)


def shards(density, operators, rates, coupling, keep_mask):
    plain = density.shape[1] == 1 and density.shape[2] == 1
    plain = plain and lax.axis_size("rows") == 2 and lax.axis_size("occa") % 2 == 0
    plain = plain and density.shape[0] * 2 == density.shape[4] and density.shape[0] % 256 == 0
    body = paired_shards if plain else general_shards
    return body(density, operators, rates, coupling, keep_mask)


def solution(mesh):
    placed = (
        P("rows", "occa", "occb", None, None),
        P(None, "rows", None),
        P(),
        P(),
        P("occa", "occb"),
    )
    return jax.shard_map(
        shards,
        mesh=mesh,
        in_specs=placed,
        out_specs=P("rows", "occa", "occb", None, None),
        check_vma=False,
    )
```

```python
import functools

import jax
import jax.numpy as jnp
from jax import lax
from jax.experimental import pallas as pl
from jax.experimental.pallas import tpu as pltpu
from jax.sharding import PartitionSpec as P

TIME_STEP = 0.05
PRECISE = lax.Precision.HIGHEST
SLOTS = 5
HALVES = 2
F32 = jnp.float32
BF16 = jnp.bfloat16


def padded(cells, sides, width):
    for axis, dim in sides:
        count = lax.axis_size(axis)
        ends = count - 1
        head = lax.slice_in_dim(cells, 0, width, axis=dim)
        tail = lax.slice_in_dim(cells, cells.shape[dim] - width, cells.shape[dim], axis=dim)
        cells = jnp.concatenate(
            [
                lax.ppermute(tail, axis, [(i, (i + 1) % count) for i in range(ends)]),
                cells,
                lax.ppermute(head, axis, [((i + 1) % count, i) for i in range(ends)]),
            ],
            axis=dim,
        )
    return cells


def neighbours(extended, count_a, count_b):
    return jnp.stack(
        [
            extended[:, 1 : count_a + 1, 1 : count_b + 1],
            extended[:, 2 : count_a + 2, 1 : count_b + 1],
            extended[:, 0:count_a, 1 : count_b + 1],
            extended[:, 1 : count_a + 1, 2 : count_b + 2],
            extended[:, 1 : count_a + 1, 0:count_b],
        ],
        axis=3,
    )


def ladder_factors(occ_a, occ_b, coupling):
    zeros = jnp.zeros_like(occ_a + occ_b)
    up_a = jnp.sqrt(occ_a + 1.0)
    up_b = jnp.sqrt(occ_b + 1.0)
    down_a = jnp.sqrt(occ_a)
    down_b = jnp.sqrt(occ_b)
    factor_re = jnp.stack(
        [zeros, zeros, down_a * coupling[0, 1], zeros, down_b * coupling[1, 1]], axis=-1
    )
    factor_im = jnp.stack(
        [zeros - 1.0, -up_a, -down_a * coupling[0, 0], -up_b, -down_b * coupling[1, 0]], axis=-1
    )
    return (factor_re, factor_im)


def weighted(stacked, factor_re, factor_im):
    part_re = stacked[..., 0, :]
    part_im = stacked[..., 1, :]
    scale_re = factor_re[None, :, :, :, None]
    scale_im = factor_im[None, :, :, :, None]
    return jnp.stack(
        [scale_re * part_re - scale_im * part_im, scale_re * part_im + scale_im * part_re], axis=4
    )


def general_shards(density, operators, rates, coupling, keep_mask):
    row_count = density.shape[0]
    count_a = density.shape[1]
    count_b = density.shape[2]
    full_ops = lax.all_gather(operators, "rows", axis=1, tiled=True)
    occ_a = (lax.axis_index("occa") * count_a + jnp.arange(count_a)).astype(F32)[:, None]
    occ_b = (lax.axis_index("occb") * count_b + jnp.arange(count_b)).astype(F32)[None, :]
    row_start = lax.axis_index("rows") * row_count
    factor_re, factor_im = ladder_factors(occ_a, occ_b, coupling)
    damping = (occ_a * rates[0] + occ_b * rates[1])[None, :, :, None, None]
    kept = keep_mask.astype(F32)[None, :, :, None, None]

    def derivative(field):
        extended = padded(field, (("occa", 1), ("occb", 2)), 1)
        stacked = neighbours(extended, count_a, count_b)
        right_ops = weighted(stacked, factor_re, -factor_im)
        right_part = jnp.einsum("iabkpc,kcm->iabpm", right_ops, full_ops, precision=PRECISE)
        left_ops = weighted(stacked, factor_re, factor_im)
        op_slice = lax.dynamic_slice_in_dim(full_ops, row_start, row_count, 2)
        left_part = lax.psum_scatter(
            jnp.einsum("kic,cabkpm->iabpm", op_slice, left_ops, precision=PRECISE),
            "rows",
            scatter_dimension=0,
            tiled=True,
        )
        return (left_part + right_part - damping * field) * kept

    start = density * kept
    first = derivative(start)
    second = derivative(first)
    return start + TIME_STEP * first + 0.5 * TIME_STEP * TIME_STEP * second


def split(value):
    high = value.astype(BF16)
    return high, (value - high.astype(F32)).astype(BF16)


def three_dots(a_high, a_low, b_high, b_low):
    dot = functools.partial(jnp.dot, preferred_element_type=F32)
    return dot(a_high, b_high) + (dot(a_high, b_low) + dot(a_low, b_high))


def row_blocks(half):
    at_row = lax.axis_index("rows")
    mine = pl.multiple_of(at_row * half, half)
    theirs = pl.multiple_of((1 - at_row) * half, half)
    return at_row, mine, theirs


def slot_operators():
    odd_a, odd_b = lax.axis_index("occa") % 2, lax.axis_index("occb") % 2
    return (0, 1 + odd_a, 2 - odd_a, 3 + odd_b, 4 - odd_b)


def begin_kernel(keep, density, operators, start0, start1, piece, sem):
    rows, _, full = density.shape
    width = full // HALVES
    half = rows // 2
    _, mine, _ = row_blocks(rows)
    odd = lax.axis_index("occa") % 2
    fetch = pltpu.make_async_copy(
        operators.at[:, pl.ds(pl.multiple_of(odd * half, half), half), pl.ds(mine, rows)],
        piece,
        sem,
    )
    fetch.start()
    kept = keep[0, 0].astype(F32)
    for part in range(2):
        for m, out in enumerate((start0, start1)):
            out[part] = density[:, part, m * width : (m + 1) * width] * kept
    fetch.wait()


def ladder_rows(rates, coupling, keep, factors):
    at_a, at_b = lax.axis_index("occa"), lax.axis_index("occb")
    lanes = (1, factors.shape[1])
    occ_a = jnp.full(lanes, at_a.astype(F32))
    occ_b = jnp.full(lanes, at_b.astype(F32))
    zero = jnp.zeros(lanes, F32)

    def above(occ):
        return zero, -jnp.sqrt(occ + 1.0)

    def below(occ, mode):
        return jnp.sqrt(occ) * coupling[mode, 1], -jnp.sqrt(occ) * coupling[mode, 0]

    rows_re, rows_im = [zero], [zero - 1.0]
    for mode, (at, occ) in enumerate(((at_a, occ_a), (at_b, occ_b))):
        even = jnp.full(lanes, at % 2) == 0
        up, down = above(occ), below(occ, mode)
        for first, second in ((up, down), (down, up)):
            rows_re.append(jnp.where(even, first[0], second[0]))
            rows_im.append(jnp.where(even, first[1], second[1]))
    damping = occ_a * rates[0] + occ_b * rates[1]
    kept = zero + keep[0, 0].astype(F32)
    for index, row in enumerate(rows_re + rows_im + [damping, kept]):
        factors[index : index + 1, :] = row


def operators_kernel(
    rates, coupling, keep, local, lp_high, lp_low, lo_high, lo_low, vr_high, vr_low, factors
):
    half = local.shape[1]
    at_row, mine, theirs = row_blocks(half)
    ladder_rows(rates, coupling, keep, factors)
    for slot, op in enumerate(slot_operators()):
        columns = pl.ds(slot * half, half)
        high, low = split(local[op])
        vr_high[at_row, slot], vr_low[at_row, slot] = high, low
        lo_high[:, columns], lo_low[:, columns] = split(local[op, :, pl.ds(mine, half)])
        lp_high[:, columns], lp_low[:, columns] = split(local[op, :, pl.ds(theirs, half)].T)


def far_kernel(local, piece, other, _high, _low, vr_high, vr_low):
    half = local.shape[1]
    quarter = piece.shape[1]
    at_row, mine, theirs = row_blocks(half)
    odd = lax.axis_index("occa") % 2
    first = pl.multiple_of(odd * quarter, quarter)
    second = pl.multiple_of((1 - odd) * quarter, quarter)
    for slot, op in enumerate(slot_operators()):
        high, low = split(local[op, :, pl.ds(theirs, half)].T)
        vr_high[1 - at_row, slot, :, pl.ds(mine, half)] = high
        vr_low[1 - at_row, slot, :, pl.ds(mine, half)] = low
        for rows, block in ((first, piece), (second, other)):
            high, low = split(block[op])
            vr_high[1 - at_row, slot, pl.ds(rows, quarter), pl.ds(theirs, half)] = high
            vr_low[1 - at_row, slot, pl.ds(rows, quarter), pl.ds(theirs, half)] = low


def left_terms(factors, fields, w_high, w_low):
    half, width = fields[0].shape[1:]
    for slot, field in enumerate(fields):
        re, im = field[0], field[1]
        scale_re = factors[slot : slot + 1, 0:1]
        scale_im = factors[SLOTS + slot : SLOTS + slot + 1, 0:1]
        rows = pl.ds(slot * half, half)
        w_high[rows, :width], w_low[rows, :width] = split(scale_re * re - scale_im * im)
        w_high[rows, width:], w_low[rows, width:] = split(scale_re * im + scale_im * re)


def right_terms(factors, fields, z_high, z_low):
    half, width = fields[0].shape[1:]
    for slot, field in enumerate(fields):
        re, im = field[0], field[1]
        scale_re = factors[slot : slot + 1, 0:1]
        scale_im = factors[SLOTS + slot : SLOTS + slot + 1, 0:1]
        columns = pl.ds(slot * width, width)
        z_high[:half, columns], z_low[:half, columns] = split(scale_re * re + scale_im * im)
        z_high[half:, columns], z_low[half:, columns] = split(scale_re * im - scale_im * re)


def closed(factors, total, arrived, field):
    damping = factors[2 * SLOTS : 2 * SLOTS + 1, 0:1]
    kept = factors[2 * SLOTS + 1 : 2 * SLOTS + 2, 0:1]
    return (total + arrived - damping * field) * kept


def taylor(start, first, second):
    return start + TIME_STEP * first + 0.5 * TIME_STEP * TIME_STEP * second


def send_kernel(factors, f0, f1, f2, f3, f4, lp_high, lp_low, out, w_high, w_low):
    width = f0.shape[2]
    left_terms(factors, (f0, f1, f2, f3, f4), w_high, w_low)
    part = three_dots(lp_high[...], lp_low[...], w_high[...], w_low[...])
    out[0] = part[:, :width]
    out[1] = part[:, width:]


def products(m, factors, fields, lo_high, lo_low, vr_high, vr_low, scratch, emit):
    w_high, w_low, z_high, z_low = scratch
    half, width = fields[0].shape[1:]
    left_terms(factors, fields, w_high, w_low)
    right_terms(factors, fields, z_high, z_low)
    deep = SLOTS * width
    far_high = vr_high[m].reshape(deep, vr_high.shape[3])
    far_low = vr_low[m].reshape(deep, vr_low.shape[3])
    right = three_dots(z_high[...], z_low[...], far_high, far_low)
    left = three_dots(lo_high[...], lo_low[...], w_high[...], w_low[...])
    for block in range(HALVES):
        for part in range(2):
            total = right[part * half : (part + 1) * half, block * width : (block + 1) * width]
            if block == m:
                total = total + left[:, part * width : (part + 1) * width]
            emit(block, part, total)


def keep_first_kernel(
    factors, f0, f1, f2, f3, f4, lo_high, lo_low, vr_high, vr_low, total0, total1, *scratch
):
    totals = (total0, total1)

    def emit(block, part, value):
        totals[block][part] = value

    products(
        0, factors, (f0, f1, f2, f3, f4), lo_high, lo_low, vr_high, vr_low, scratch, emit
    )


def keep_last_kernel(
    last, factors, f0, f1, f2, f3, f4, lo_high, lo_low, vr_high, vr_low, before0, before1,
    arrived0, field0, *rest
):
    start0, (out0, total1, *scratch) = (rest[0], rest[1:]) if last else (None, rest)

    def emit(block, part, value):
        if block == 1:
            total1[part] = value + before1[part]
        else:
            change = closed(factors, value + before0[part], arrived0[part], field0[part])
            out0[part] = taylor(start0[part], field0[part], change) if last else change

    products(
        1, factors, (f0, f1, f2, f3, f4), lo_high, lo_low, vr_high, vr_low, scratch, emit
    )


def close_kernel(factors, total, arrived, field, out):
    for part in range(2):
        out[part] = closed(factors, total[part], arrived[part], field[part])


def end_kernel(factors, total, arrived, field, start, out0, out):
    width = start.shape[2]
    for part in range(2):
        change = closed(factors, total[part], arrived[part], field[part])
        out[:, part, :width] = out0[part]
        out[:, part, width:] = taylor(start[part], field[part], change)


VMEM_SPEC = pl.BlockSpec(memory_space=pltpu.VMEM)
SMEM_SPEC = pl.BlockSpec(memory_space=pltpu.SMEM)
ANY_SPEC = pl.BlockSpec(memory_space=pl.ANY)


def call(kernel, outs, args, specs, name, flops=0, scratch=(), mib=16, aliases=None):
    moved = sum(a.size * a.dtype.itemsize for a in args)
    return pl.pallas_call(
        kernel,
        out_shape=outs,
        in_specs=specs,
        out_specs=jax.tree.map(lambda _: VMEM_SPEC, outs),
        scratch_shapes=scratch,
        input_output_aliases=aliases or {},
        compiler_params=pltpu.CompilerParams(vmem_limit_bytes=mib << 20),
        cost_estimate=pl.CostEstimate(flops=flops, bytes_accessed=moved, transcendentals=0),
        name=name,
    )(*args)


def paired_shards(density, operators, rates, coupling, keep_mask):
    rows = density.shape[0]
    full = density.shape[4]
    width = full // HALVES
    deep = SLOTS * rows
    count_a, count_b = lax.axis_size("occa"), lax.axis_size("occb")

    def swaps(first, count):
        ups = [(i, i + 1) for i in range(first, count - 1, 2)]
        return ups + [(j, i) for i, j in ups]

    links = (
        ("occa", swaps(0, count_a)),
        ("occa", swaps(1, count_a)),
        ("occb", swaps(0, count_b)),
        ("occb", swaps(1, count_b)),
    )
    over_rows = swaps(0, 2)

    def shape(*dims, dtype=F32):
        return jax.ShapeDtypeStruct(dims, dtype)

    block = shape(2, rows, width)
    start0, start1, piece = call(
        begin_kernel,
        (block, block, shape(SLOTS, rows // 2, rows)),
        (keep_mask, density.reshape(rows, 2, full), operators),
        [SMEM_SPEC, VMEM_SPEC, ANY_SPEC],
        "begin",
        scratch=[pltpu.SemaphoreType.DMA(())],
    )
    start = (start0, start1)

    piece = lax.ppermute(piece, "rows", over_rows)
    other = lax.ppermute(piece, "occa", links[0][1])

    wide = shape(rows, deep, dtype=BF16)
    tall = shape(2, SLOTS, rows, full, dtype=BF16)
    *sides, vr_high, vr_low, factors = call(
        operators_kernel,
        (wide,) * 4 + (tall,) * 2 + (shape(16, 128),),
        (rates, coupling, keep_mask, operators),
        [SMEM_SPEC] * 3 + [VMEM_SPEC],
        "prepare_operators",
        mib=20,
    )
    lp, lo = sides[:2], sides[2:]
    vr = call(
        far_kernel,
        (tall,) * 2,
        (operators, piece, other, vr_high, vr_low),
        [VMEM_SPEC] * 5,
        "prepare_far",
        mib=20,
        aliases={3: 0, 4: 1},
    )

    w_scratch = [pltpu.VMEM((deep, 2 * width), BF16)] * 2
    z_scratch = [pltpu.VMEM((2 * rows, SLOTS * width), BF16)] * 2
    unit = 6 * rows * deep * 2 * width

    def derivative(field, last):
        fields, arrived = [], []
        for m in range(HALVES):
            fields.append((field[m],) + tuple(lax.ppermute(field[m], *link) for link in links))
            args = (factors, *fields[m], *lp)
            sent = call(
                send_kernel, block, args, [VMEM_SPEC] * len(args), "send_part", unit, w_scratch
            )
            arrived.append(lax.ppermute(sent, "rows", over_rows))
        args = (factors, *fields[0], *lo, *vr)
        before = call(
            keep_first_kernel,
            (block, block),
            args,
            [VMEM_SPEC] * len(args),
            "keep_first",
            3 * unit,
            w_scratch + z_scratch,
            24,
        )
        args = (factors, *fields[1], *lo, *vr, *before, arrived[0], field[0])
        args += (start[0],) if last else ()
        ready, total = call(
            functools.partial(keep_last_kernel, last),
            (block, block),
            args,
            [VMEM_SPEC] * len(args),
            "keep_last",
            3 * unit,
            w_scratch + z_scratch,
            24,
        )
        return ready, (total, arrived[1], field[1])

    first0, args = derivative(start, False)
    first1 = call(close_kernel, block, (factors, *args), [VMEM_SPEC] * 4, "close")
    ready, args = derivative((first0, first1), True)
    result = call(
        end_kernel,
        shape(rows, 2, full),
        (factors, *args, start[1], ready),
        [VMEM_SPEC] * 6,
        "end",
    )
    return result.reshape(density.shape)


def shards(density, operators, rates, coupling, keep_mask):
    plain = density.shape[1] == 1 and density.shape[2] == 1
    plain = plain and lax.axis_size("rows") == 2 and lax.axis_size("occa") % 2 == 0
    plain = plain and density.shape[0] * 2 == density.shape[4] and density.shape[0] % 256 == 0
    body = paired_shards if plain else general_shards
    return body(density, operators, rates, coupling, keep_mask)


def solution(mesh):
    placed = (
        P("rows", "occa", "occb", None, None),
        P(None, "rows", None),
        P(),
        P(),
        P("occa", "occb"),
    )
    return jax.shard_map(
        shards,
        mesh=mesh,
        in_specs=placed,
        out_specs=P("rows", "occa", "occb", None, None),
        check_vma=False,
    )
```

```python
import functools

import jax
import jax.numpy as jnp
from jax import lax
from jax.experimental import pallas as pl
from jax.experimental.pallas import tpu as pltpu
from jax.sharding import PartitionSpec as P


TIME_STEP = 0.05
PRECISE = lax.Precision.HIGHEST
SLOTS = 5
NEAR = 2
HALVES = 2
F32 = jnp.float32
BF16 = jnp.bfloat16


def padded(cells, sides, width):
    for axis, dim in sides:
        count = lax.axis_size(axis)
        ends = count - 1
        head = lax.slice_in_dim(cells, 0, width, axis=dim)
        tail = lax.slice_in_dim(cells, cells.shape[dim] - width, cells.shape[dim], axis=dim)
        cells = jnp.concatenate(
            [
                lax.ppermute(tail, axis, [(i, (i + 1) % count) for i in range(ends)]),
                cells,
                lax.ppermute(head, axis, [((i + 1) % count, i) for i in range(ends)]),
            ],
            axis=dim,
        )
    return cells


def neighbours(extended, count_a, count_b):
    return jnp.stack(
        [
            extended[:, 1 : count_a + 1, 1 : count_b + 1],
            extended[:, 2 : count_a + 2, 1 : count_b + 1],
            extended[:, 0:count_a, 1 : count_b + 1],
            extended[:, 1 : count_a + 1, 2 : count_b + 2],
            extended[:, 1 : count_a + 1, 0:count_b],
        ],
        axis=3,
    )


def ladder_factors(occ_a, occ_b, coupling):
    zeros = jnp.zeros_like(occ_a + occ_b)
    up_a = jnp.sqrt(occ_a + 1.0)
    up_b = jnp.sqrt(occ_b + 1.0)
    down_a = jnp.sqrt(occ_a)
    down_b = jnp.sqrt(occ_b)
    factor_re = jnp.stack(
        [zeros, zeros, down_a * coupling[0, 1], zeros, down_b * coupling[1, 1]], axis=-1
    )
    factor_im = jnp.stack(
        [zeros - 1.0, -up_a, -down_a * coupling[0, 0], -up_b, -down_b * coupling[1, 0]], axis=-1
    )
    return (factor_re, factor_im)


def weighted(stacked, factor_re, factor_im):
    part_re = stacked[..., 0, :]
    part_im = stacked[..., 1, :]
    scale_re = factor_re[None, :, :, :, None]
    scale_im = factor_im[None, :, :, :, None]
    return jnp.stack(
        [scale_re * part_re - scale_im * part_im, scale_re * part_im + scale_im * part_re], axis=4
    )


def general_shards(density, operators, rates, coupling, keep_mask):
    row_count = density.shape[0]
    count_a = density.shape[1]
    count_b = density.shape[2]
    full_ops = lax.all_gather(operators, "rows", axis=1, tiled=True)
    occ_a = (lax.axis_index("occa") * count_a + jnp.arange(count_a)).astype(F32)[:, None]
    occ_b = (lax.axis_index("occb") * count_b + jnp.arange(count_b)).astype(F32)[None, :]
    row_start = lax.axis_index("rows") * row_count
    factor_re, factor_im = ladder_factors(occ_a, occ_b, coupling)
    damping = (occ_a * rates[0] + occ_b * rates[1])[None, :, :, None, None]
    kept = keep_mask.astype(F32)[None, :, :, None, None]

    def derivative(field):
        extended = padded(field, (("occa", 1), ("occb", 2)), 1)
        stacked = neighbours(extended, count_a, count_b)
        right_ops = weighted(stacked, factor_re, -factor_im)
        right_part = jnp.einsum("iabkpc,kcm->iabpm", right_ops, full_ops, precision=PRECISE)
        left_ops = weighted(stacked, factor_re, factor_im)
        op_slice = lax.dynamic_slice_in_dim(full_ops, row_start, row_count, 2)
        left_part = lax.psum_scatter(
            jnp.einsum("kic,cabkpm->iabpm", op_slice, left_ops, precision=PRECISE),
            "rows",
            scatter_dimension=0,
            tiled=True,
        )
        return (left_part + right_part - damping * field) * kept

    start = density * kept
    first = derivative(start)
    second = derivative(first)
    return start + TIME_STEP * first + 0.5 * TIME_STEP * TIME_STEP * second


def split(value):
    high = value.astype(BF16)
    return high, (value - high.astype(F32)).astype(BF16)


def three_dots(a_high, a_low, b_high, b_low):
    dot = functools.partial(jnp.dot, preferred_element_type=F32)
    return dot(a_high, b_high) + (dot(a_high, b_low) + dot(a_low, b_high))


def row_blocks(half):
    at_row = lax.axis_index("rows")
    mine = pl.multiple_of(at_row * half, half)
    theirs = pl.multiple_of((1 - at_row) * half, half)
    return at_row, mine, theirs


def slot_operators():
    odd_a, odd_b = lax.axis_index("occa") % 2, lax.axis_index("occb") % 2
    return (0, 1 + odd_a, 2 - odd_a, 3 + odd_b, 4 - odd_b)


def masked_half(m, keep, density, out, raw, sem):
    width = out.shape[2]
    copy = pltpu.make_async_copy(density.at[:, :, m * width : (m + 1) * width], raw, sem)
    copy.start()

    def finish():
        kept = keep[0, 0].astype(F32)
        copy.wait()
        for part in range(2):
            out[part] = raw[:, part, :] * kept

    return finish


def begin_kernel(keep, density, operators, out, piece, raw, sem, piece_sems):
    rows = density.shape[0]
    quarter = rows // 2
    eighth = quarter // 2
    _, mine, _ = row_blocks(rows)
    odd = lax.axis_index("occa") % 2
    down = pl.multiple_of(odd * quarter, quarter)
    finish = masked_half(0, keep, density, out, raw, sem)
    square = pltpu.make_async_copy(
        operators.at[:, pl.ds(down, quarter), pl.ds(pl.multiple_of(mine + down, quarter), quarter)],
        piece.at[:, :quarter],
        piece_sems.at[0],
    )
    corner = pltpu.make_async_copy(
        operators.at[
            :,
            pl.ds(pl.multiple_of(odd * eighth, eighth), eighth),
            pl.ds(pl.multiple_of(mine + quarter, quarter), quarter),
        ],
        piece.at[:, quarter:],
        piece_sems.at[1],
    )
    square.start()
    corner.start()
    finish()
    square.wait()
    corner.wait()


def begin_rest_kernel(keep, density, first, out, both, raw, sem):
    finish = masked_half(1, keep, density, out, raw, sem)
    both[0] = first[...]
    finish()
    both[1] = out[...]


def ladder_rows(rates, coupling, keep, factors):
    at_a, at_b = lax.axis_index("occa"), lax.axis_index("occb")
    lanes = (1, factors.shape[1])
    occ_a = jnp.full(lanes, at_a.astype(F32))
    occ_b = jnp.full(lanes, at_b.astype(F32))
    zero = jnp.zeros(lanes, F32)

    def above(at, occ, count):
        inside = jnp.full(lanes, at) < count - 1
        return zero, jnp.where(inside, -jnp.sqrt(occ + 1.0), 0.0)

    def below(occ, mode):
        return jnp.sqrt(occ) * coupling[mode, 1], -jnp.sqrt(occ) * coupling[mode, 0]

    rows_re, rows_im = [zero], [zero - 1.0]
    counts = lax.axis_size("occa"), lax.axis_size("occb")
    for mode, (at, occ) in enumerate(((at_a, occ_a), (at_b, occ_b))):
        even = jnp.full(lanes, at % 2) == 0
        up, down = above(at, occ, counts[mode]), below(occ, mode)
        for first, second in ((up, down), (down, up)):
            rows_re.append(jnp.where(even, first[0], second[0]))
            rows_im.append(jnp.where(even, first[1], second[1]))
    damping = occ_a * rates[0] + occ_b * rates[1]
    kept = zero + keep[0, 0].astype(F32)
    for index, row in enumerate(rows_re + rows_im + [damping, kept]):
        factors[index : index + 1, :] = row


def operators_kernel(
    rates, coupling, keep, local, lp_high, lp_low, lo_high, lo_low, vr_high, vr_low, factors
):
    half = local.shape[1]
    at_row, mine, theirs = row_blocks(half)
    ladder_rows(rates, coupling, keep, factors)
    for slot, op in enumerate(slot_operators()):
        columns = pl.ds(slot * half, half)
        high, low = split(local[op])
        vr_high[at_row, slot], vr_low[at_row, slot] = high, low
        lo_high[:, columns], lo_low[:, columns] = split(local[op, :, pl.ds(mine, half)])
        lp_high[:, columns], lp_low[:, columns] = split(local[op, :, pl.ds(theirs, half)].T)


def far_kernel(local, piece, other, _high, _low, vr_high, vr_low, corner):
    half = local.shape[1]
    quarter = half // 2
    eighth = quarter // 2
    at_row, mine, theirs = row_blocks(half)
    odd = lax.axis_index("occa") % 2

    def put(slot, rows, columns, count, value):
        columns = pl.ds(pl.multiple_of(columns, quarter), value.shape[1])
        rows = pl.ds(rows, count)
        vr_high[1 - at_row, slot, rows, columns], vr_low[1 - at_row, slot, rows, columns] = split(
            value
        )

    for slot, op in enumerate(slot_operators()):
        put(slot, 0, mine, half, local[op, :, pl.ds(theirs, half)].T)
        for place, block in ((odd, piece), (1 - odd, other)):
            down = pl.multiple_of(place * quarter, quarter)
            put(slot, down, theirs + down, quarter, block[op, :quarter])
            corner[pl.ds(pl.multiple_of(place * eighth, eighth), eighth)] = block[op, quarter:]
        above = corner[...]
        put(slot, 0, theirs + quarter, quarter, above)
        put(slot, quarter, theirs, quarter, above.T)


def left_terms(factors, fields, w_high, w_low, base=0):
    half, width = fields[0].shape[1:]
    for index, field in enumerate(fields):
        slot = base + index
        re, im = field[0], field[1]
        scale_re = factors[slot : slot + 1, 0:1]
        scale_im = factors[SLOTS + slot : SLOTS + slot + 1, 0:1]
        rows = pl.ds(index * half, half)
        w_high[rows, :width], w_low[rows, :width] = split(scale_re * re - scale_im * im)
        w_high[rows, width:], w_low[rows, width:] = split(scale_re * im + scale_im * re)


def right_terms(factors, fields, z_high, z_low):
    half, width = fields[0].shape[1:]
    for slot, field in enumerate(fields):
        re, im = field[0], field[1]
        scale_re = factors[slot : slot + 1, 0:1]
        scale_im = factors[SLOTS + slot : SLOTS + slot + 1, 0:1]
        columns = pl.ds(slot * width, width)
        z_high[:half, columns], z_low[:half, columns] = split(scale_re * re + scale_im * im)
        z_high[half:, columns], z_low[half:, columns] = split(scale_re * im - scale_im * re)


def closed(factors, total, arrived, field):
    damping = factors[2 * SLOTS : 2 * SLOTS + 1, 0:1]
    kept = factors[2 * SLOTS + 1 : 2 * SLOTS + 2, 0:1]
    return (total + arrived - damping * field) * kept


def taylor(start, first, second):
    return start + TIME_STEP * first + 0.5 * TIME_STEP * TIME_STEP * second


def half_of(m, fields):
    return [field.at[m] if len(field.shape) == 4 else field for field in fields]


def send_near_kernel(m, factors, f0, f1, lp_high, lp_low, out, w_high, w_low):
    width = f0.shape[2]
    deep = NEAR * f0.shape[1]
    left_terms(factors, half_of(m, (f0, f1)), w_high, w_low)
    part = three_dots(lp_high[:, :deep], lp_low[:, :deep], w_high[...], w_low[...])
    out[0] = part[:, :width]
    out[1] = part[:, width:]


def send_kernel(factors, f2, f3, f4, lp_high, lp_low, before, out, w_high, w_low):
    width = f2.shape[2]
    deep = NEAR * f2.shape[1]
    left_terms(factors, (f2, f3, f4), w_high, w_low, NEAR)
    part = three_dots(lp_high[:, deep:], lp_low[:, deep:], w_high[...], w_low[...])
    out[0] = part[:, :width] + before[0]
    out[1] = part[:, width:] + before[1]


def right_rows(m, vr, columns):
    deep = vr.shape[1] * vr.shape[2]
    return vr[m, :, :, columns].reshape(deep, columns.stop - columns.start)


def keep_early_kernel(
    factors, f0, f1, f2, f3, f4, lo_high, lo_low, vr_high, vr_low, *rest
):
    total0, total1, w_high, w_low, z_high, z_low = rest
    fields = half_of(0, (f0, f1, f2, f3, f4))
    half, width = f0.shape[1:]
    left_terms(factors, fields, w_high, w_low)
    right_terms(factors, fields, z_high, z_low)
    whole = slice(0, HALVES * width)
    right = three_dots(
        z_high[...], z_low[...], right_rows(0, vr_high, whole), right_rows(0, vr_low, whole)
    )
    left = three_dots(lo_high[...], lo_low[...], w_high[...], w_low[...])
    for part in range(2):
        rows, columns = slice(part * half, (part + 1) * half), slice(part * width, (part + 1) * width)
        total0[part] = right[rows, :width] + left[:, columns]
        total1[part] = right[rows, width:]


def keep_late_kernel(factors, f0, f1, f2, f3, f4, vr_high, vr_low, before, total, z_high, z_low):
    fields = half_of(1, (f0, f1, f2, f3, f4))
    half, width = f0.shape[1:]
    right_terms(factors, fields, z_high, z_low)
    first = slice(0, width)
    right = three_dots(
        z_high[...], z_low[...], right_rows(1, vr_high, first), right_rows(1, vr_low, first)
    )
    for part in range(2):
        total[part] = before[part] + right[part * half : (part + 1) * half]


def keep_rest_kernel(
    factors, f0, f1, f2, f3, f4, lo_high, lo_low, vr_high, vr_low, before, z_high, z_low, total,
    w_high, w_low,
):
    fields = half_of(1, (f0, f1, f2, f3, f4))
    half, width = f0.shape[1:]
    left_terms(factors, fields, w_high, w_low)
    second = slice(width, HALVES * width)
    right = three_dots(
        z_high[...], z_low[...], right_rows(1, vr_high, second), right_rows(1, vr_low, second)
    )
    left = three_dots(lo_high[...], lo_low[...], w_high[...], w_low[...])
    for part in range(2):
        rows, columns = slice(part * half, (part + 1) * half), slice(part * width, (part + 1) * width)
        total[part] = before[part] + (right[rows] + left[:, columns])


def close_kernel(factors, total, arrived, field, out):
    for part in range(2):
        out[part] = closed(factors, total[part], arrived[part], field[part])


def end_kernel(m, factors, total, arrived, field, start, *rest):
    out, packed, sems = rest[-3:]
    rows, width = start.shape[1:]
    columns = slice(m * width, (m + 1) * width)
    stores = []
    for index in range(2):
        span = slice(index * (rows // 2), (index + 1) * (rows // 2))
        for part in range(2):
            change = closed(factors, total[part, span], arrived[part, span], field[part, span])
            packed[span, part, :] = taylor(start[part, span], field[part, span], change)
        stores.append(
            pltpu.make_async_copy(packed.at[span], out.at[span, :, columns], sems.at[index])
        )
        stores[-1].start()
    for store in stores:
        store.wait()


VMEM_SPEC = pl.BlockSpec(memory_space=pltpu.VMEM)
SMEM_SPEC = pl.BlockSpec(memory_space=pltpu.SMEM)
ANY_SPEC = pl.BlockSpec(memory_space=pl.ANY)


def call(kernel, outs, args, specs, flops=0, scratch=(), mib=16, aliases=None, placed=VMEM_SPEC):
    moved = sum(a.size * a.dtype.itemsize for a in args)
    return run(kernel, outs, args, specs, flops, scratch, mib, aliases, placed, moved)


def run(kernel, outs, args, specs, flops, scratch, mib, aliases, placed, moved):
    return pl.pallas_call(
        kernel,
        out_shape=outs,
        in_specs=specs,
        out_specs=jax.tree.map(lambda _: placed, outs),
        scratch_shapes=scratch,
        input_output_aliases=aliases or {},
        compiler_params=pltpu.CompilerParams(vmem_limit_bytes=mib << 20),
        cost_estimate=pl.CostEstimate(flops=flops, bytes_accessed=moved, transcendentals=0),
    )(*args)


def paired_shards(density, operators, rates, coupling, keep_mask):
    rows = density.shape[0]
    full = density.shape[4]
    width = full // HALVES
    deep = SLOTS * rows
    count_a, count_b = lax.axis_size("occa"), lax.axis_size("occb")

    def swaps(first, count):
        ups = [(i, i + 1) for i in range(first, count - 1, 2)]
        return ups + [(j, i) for i, j in ups]

    def swaps_b(first):
        along = swaps(first, count_b)
        alone = set(range(count_b)) - {i for i, _ in along}
        at = [(a * count_b + i, a * count_b + j) for a in range(count_a) for i, j in along]
        inner = swaps(0, count_a)
        return at + [(i * count_b + b, j * count_b + b) for b in sorted(alone) for i, j in inner]

    links = (
        ("a_pair", "occa", swaps(0, count_a)),
        ("a_gap", "occa", swaps(1, count_a)),
        ("b_pair", ("occa", "occb"), swaps_b(0)),
        ("b_gap", ("occa", "occb"), swaps_b(1)),
    )
    over_rows = swaps(0, 2)

    def shape(*dims, dtype=F32):
        return jax.ShapeDtypeStruct(dims, dtype)

    block = shape(2, rows, width)
    in_hbm = functools.partial(pltpu.with_memory_space_constraint, memory_space=pltpu.HBM)
    cells = keep_mask, in_hbm(density.reshape(rows, 2, full))
    half_scratch = [pltpu.VMEM((rows, 2, width), F32), pltpu.SemaphoreType.DMA(())]
    start0, piece = call(
        begin_kernel,
        (block, shape(SLOTS, 3 * (rows // 4), rows // 2)),
        (*cells, in_hbm(operators)),
        [SMEM_SPEC, ANY_SPEC, ANY_SPEC],
        scratch=half_scratch + [pltpu.SemaphoreType.DMA((2,))],
    )
    start1, both = call(
        begin_rest_kernel,
        (block, shape(HALVES, 2, rows, width)),
        (*cells, start0),
        [SMEM_SPEC, ANY_SPEC, VMEM_SPEC],
        scratch=half_scratch,
    )
    start = (start0, start1)

    piece = lax.ppermute(piece, "rows", over_rows)
    other = lax.ppermute(piece, "occa", links[0][2])

    wide = shape(rows, deep, dtype=BF16)
    tall = shape(2, SLOTS, rows, full, dtype=BF16)
    *sides, vr_high, vr_low, factors = call(
        operators_kernel,
        (wide,) * 4 + (tall,) * 2 + (shape(16, 128),),
        (rates, coupling, keep_mask, operators),
        [SMEM_SPEC] * 3 + [VMEM_SPEC],
        mib=20,
    )
    lp, lo = sides[:2], sides[2:]
    vr = call(
        far_kernel,
        (tall,) * 2,
        (operators, piece, other, vr_high, vr_low),
        [VMEM_SPEC] * 5,
        mib=20,
        aliases={3: 0, 4: 1},
        scratch=[pltpu.VMEM((rows // 2, rows // 2), F32)],
    )

    terms = shape(2 * rows, SLOTS * width, dtype=BF16)
    w_scratch = [pltpu.VMEM((deep, 2 * width), BF16)] * 2
    z_scratch = [pltpu.VMEM(terms.shape, BF16)] * 2
    unit = 6 * rows * deep * 2 * width

    def move(values, link):
        _, axis, swap = link
        return lax.ppermute(values, axis, swap)

    def kernel(body, outs, args, units, scratch, mib=16):
        return call(body, outs, args, [VMEM_SPEC] * len(args), units * unit, scratch, mib)

    def derivative(field, both):
        pair = None if both is None else move(both, links[0])
        fields, arrived = [], []
        for m in range(HALVES):
            moved = [move(field[m], link) for link in links[1:]]
            beside = move(field[m], links[0]) if pair is None else pair
            fields.append((field[m], beside, *moved))
            near = kernel(
                functools.partial(send_near_kernel, m),
                block,
                (factors, *fields[m][:NEAR], *lp),
                1,
                [pltpu.VMEM((NEAR * rows, 2 * width), BF16)] * 2,
            )
            sent = kernel(
                send_kernel,
                block,
                (factors, *fields[m][NEAR:], *lp, near),
                1,
                [pltpu.VMEM(((SLOTS - NEAR) * rows, 2 * width), BF16)] * 2,
            )
            arrived.append(lax.ppermute(sent, "rows", over_rows))
        total0, total1 = kernel(
            keep_early_kernel,
            (block, block),
            (factors, *fields[0], *lo, *vr),
            3,
            w_scratch + z_scratch,
            24,
        )
        total0, *z = kernel(
            keep_late_kernel, (block, terms, terms), (factors, *fields[1], *vr, total0), 1, ()
        )
        total1 = kernel(
            keep_rest_kernel, block, (factors, *fields[1], *lo, *vr, total1, *z), 2, w_scratch, 24
        )
        return list(zip((total0, total1), arrived, field))

    early, late = derivative(start, both)
    first0 = kernel(close_kernel, block, (factors, *early), 0, ())
    first1 = kernel(close_kernel, block, (factors, *late), 0, ())
    result = ()
    for m, args in enumerate(derivative((first0, first1), None)):
        result = (
            call(
                functools.partial(end_kernel, m),
                shape(rows, 2, full),
                (factors, *args, start[m], *result),
                [VMEM_SPEC] * 5 + [ANY_SPEC] * len(result),
                scratch=[pltpu.VMEM((rows, 2, width), F32), pltpu.SemaphoreType.DMA((2,))],
                aliases={5: 0} if result else None,
                placed=ANY_SPEC,
            ),
        )
    (result,) = result
    return result.reshape(density.shape)


def shards(density, operators, rates, coupling, keep_mask):
    plain = density.shape[1] == 1 and density.shape[2] == 1
    plain = plain and lax.axis_size("rows") == 2 and lax.axis_size("occa") % 2 == 0
    plain = plain and density.shape[0] * 2 == density.shape[4] and density.shape[0] % 256 == 0
    if not plain:
        return general_shards(density, operators, rates, coupling, keep_mask)
    return paired_shards(density, operators, rates, coupling, keep_mask)


def solution(mesh):
    placed = (
        P("rows", "occa", "occb", None, None),
        P(None, "rows", None),
        P(),
        P(),
        P("occa", "occb"),
    )
    return jax.shard_map(
        shards,
        mesh=mesh,
        in_specs=placed,
        out_specs=P("rows", "occa", "occb", None, None),
        check_vma=False,
    )
```
